32 devices in a mesh: tile: 8 (over z, x), group: 4 (over y, core).
Axes of the slice: x: 2, y: 2, z: 4, core: 2. Of those that a mesh axis runs over, the one named last changes fastest.
Arguments:
- features: bfloat16 [4, 512, 32, 256], P('group', 'tile'), may hold values from -6 to 6
- out_grad: bfloat16 [4, 96, 14, 14, 256], P('group', 'tile'), may hold values from -6 to 6
- pair_count: int32 [4, 8, 8], P('group'), may hold values from 0 to 2, as said below
- sample_grid: int32 [4, 8, 8, 2, 4, 14], P('group', 'tile'), may hold values from 0 to 62, as said below
- first_kernel: bfloat16 [3, 3, 256, 256], replicated, may hold values from -0.125 to 0.125
- second_kernel: bfloat16 [3, 3, 256, 256], replicated, may hold values from -0.125 to 0.125
Outputs:
- feature_grad: bfloat16 [4, 512, 32, 256], P('group', 'tile')
- first_grad: float32 [3, 3, 256, 256], replicated
- second_grad: float32 [3, 3, 256, 256], replicated
The draws below stay inside these ranges and needn't reach their ends.
Inputs may be any that keep to these rules, and one draw needn't show every extreme that they name: Every entry is at most 2; in every scene each reader t has pair_count entries summing to exactly 12 over the owners, and every reader has some owner sending it exactly 2 regions. `sample_grid`: lower row indices are at most 62 and lower column indices at most 30; fractions lie in 0 to 15; along a slot's samples the positions (16 * lower index + fraction) ascend with a constant step of 8 to 64.
All inputs are finite; a program needn't handle non-finite values.
Results may differ from the reference program's by a relative error of at most 0.015.
Values may be sent and summed in bfloat16 or wider, within the bound.
No kernel may reach another device: no remote copies, remote signals or barrier semaphores. Data moves between devices by JAX's collectives and lax.ppermute only.
A program may use at most 256 MiB of HBM per device.

```python
import math
import jax
import jax.numpy as jnp
from jax import lax

C = 256
RES = 14
TH = 64
TW = 32
CAP = 2
R_DEV = 12
SCENES = 4
READS = 96
ROWS = 512
N_TILE = 8


def draw_pair_count(key, part):
    doubled = max(1, R_DEV // 4, R_DEV - N_TILE)
    chosen_count = R_DEV - doubled

    def one_scene(scene_key):
        heat_key, noise_key = jax.random.split(scene_key)
        heat_level = jax.random.randint(heat_key, (N_TILE,), 0, 4)
        noise_draw = jax.random.randint(noise_key, (N_TILE, N_TILE), 0, 1048576)
        owners = jnp.arange(N_TILE, dtype=jnp.int32)
        owner_score = (noise_draw + heat_level[None, :] * 524288) * 128 + owners[None, :]
        owner_rank = jnp.sum((owner_score[:, None, :] > owner_score[:, :, None]).astype(jnp.int32), axis=2)
        counts = (owner_rank < chosen_count).astype(jnp.int32) + (owner_rank < doubled).astype(jnp.int32)
        return counts.T
    return jax.vmap(one_scene)(jax.random.split(key, SCENES))


def draw_sample_grid(key, part):
    base_shape = (SCENES, N_TILE, N_TILE, CAP)
    steps_along = jnp.arange(RES, dtype=jnp.int32)

    def one_axis(axis_key, extent):
        step_key, start_key = jax.random.split(axis_key)
        stride_top = min(64, ((extent - 1) * 16 - 1) // (RES - 1))
        stride = jax.random.randint(step_key, base_shape, 8, stride_top + 1)
        anchor = jax.random.randint(start_key, base_shape, 0, (extent - 1) * 16 - (RES - 1) * stride)
        places = anchor[..., None] + stride[..., None] * steps_along
        return (places // 16, places % 16)
    row_key, col_key = jax.random.split(key)
    row_low, row_frac = one_axis(row_key, TH)
    col_low, col_frac = one_axis(col_key, TW)
    return jnp.stack([row_low, row_frac, col_low, col_frac], axis=-2).astype(jnp.int32)


def block_scale(own_key, shape, shards, low, high):
    level = 1.0
    for position, parts in shards:
        heights = jax.random.uniform(jax.random.fold_in(jax.random.fold_in(own_key, 6), position), (parts,), jnp.float32, low / len(shards), high / len(shards))
        level = level * jnp.repeat(jnp.exp(heights), shape[position] // parts).reshape((-1,) + (1,) * (len(shape) - 1 - position))
    return level


def noise(stream_key, shape, width, reach, cuts=(), kind=jnp.bfloat16):
    values = width * jax.random.normal(stream_key, shape, jnp.float32)
    if cuts:
        values = values * block_scale(stream_key, shape, cuts, -0.22, 0.18)
    return jnp.clip(values, -reach, reach).astype(kind)


def setup_inputs(seed: int = 0) -> dict:
    splits = jax.random.split(jax.random.key(seed), 7)
    features = noise(splits[0], (SCENES, ROWS, TW, C), 1.0, 6.0, ((0, 4), (1, 8)))
    out_grad = noise(splits[1], (SCENES, READS, RES, RES, C), 1.0, 6.0, ((0, 4), (1, 8)))
    pair_count = draw_pair_count(jax.random.fold_in(splits[6], 71), 0)
    sample_grid = draw_sample_grid(jax.random.fold_in(splits[6], 71), 0)
    first_kernel = noise(splits[4], (3, 3, C, C), (9 * C) ** -0.5, 0.125)
    second_kernel = noise(splits[5], (3, 3, C, C), (9 * C) ** -0.5, 0.125)
    return dict(features=features, out_grad=out_grad, pair_count=pair_count, sample_grid=sample_grid, first_kernel=first_kernel, second_kernel=second_kernel)


def interp_weights(lower_index, fraction, extent):
    places = jnp.arange(extent, dtype=jnp.int32)
    upper_share = fraction.astype(jnp.float32) / 16.0
    lower_part = jnp.where(places == lower_index[..., None], 1.0 - upper_share[..., None], 0.0)
    upper_part = jnp.where(places == lower_index[..., None] + 1, upper_share[..., None], 0.0)
    return lower_part + upper_part

def slot_weights(slot_grid, active, height, across):
    row_weights = interp_weights(slot_grid[..., 0, :], slot_grid[..., 1, :], height)
    row_weights = row_weights * active[..., None, None].astype(jnp.float32)
    col_weights = interp_weights(slot_grid[..., 2, :], slot_grid[..., 3, :], across)
    return (row_weights.astype(jnp.bfloat16), col_weights.astype(jnp.bfloat16))

def sample_blocks(tile_image, row_weights, col_weights):
    leading = row_weights.shape[:2]
    slot_total = leading[0] * leading[1]
    extent = row_weights.shape[2]
    row_blocks = row_weights.reshape(slot_total // 8, 8, extent, row_weights.shape[3])
    col_blocks = col_weights.reshape(slot_total // 8, 8, extent, col_weights.shape[3])
    image_wide = tile_image.astype(jnp.float32)

    def one_block(members):
        row_part, col_part = members
        stripes = jnp.einsum('spy,yxc->spxc', row_part.astype(jnp.float32), image_wide).astype(jnp.bfloat16)
        return jnp.einsum('sqx,spxc->spqc', col_part.astype(jnp.float32), stripes.astype(jnp.float32)).astype(jnp.bfloat16)
    sampled = lax.map(one_block, (row_blocks, col_blocks))
    return sampled.reshape(leading + (extent, extent, tile_image.shape[2]))

def spread_blocks(slot_grads, row_weights, col_weights):
    leading = row_weights.shape[:2]
    slot_total = leading[0] * leading[1]
    extent = row_weights.shape[2]
    height = row_weights.shape[3]
    across = col_weights.shape[3]
    channels = slot_grads.shape[-1]
    row_blocks = row_weights.reshape(slot_total // 8, 8, extent, height)
    col_blocks = col_weights.reshape(slot_total // 8, 8, extent, across)
    grad_blocks = slot_grads.reshape(slot_total // 8, 8, extent, extent, channels)

    def one_block(running_sum, members):
        row_part, col_part, grad_part = members
        stripes = jnp.einsum('sqx,spqc->spxc', col_part.astype(jnp.float32), grad_part.astype(jnp.float32)).astype(jnp.bfloat16)
        added = jnp.einsum('spy,spxc->yxc', row_part.astype(jnp.float32), stripes.astype(jnp.float32))
        return (running_sum + added, None)
    initial = jnp.zeros((height, across, channels), jnp.float32)
    summed, unused = lax.scan(one_block, initial, (row_blocks, col_blocks, grad_blocks))
    return summed.astype(jnp.bfloat16)

def unfold(values):
    region_count = values.shape[0]
    extent = values.shape[1]
    channels = values.shape[3]
    padded = jnp.pad(values, ((0, 0), (1, 1), (1, 1), (0, 0)))
    pieces = [padded[:, row_off:row_off + extent, col_off:col_off + extent, :] for row_off in range(3) for col_off in range(3)]
    return jnp.concatenate(pieces, axis=-1).reshape(region_count * extent * extent, 9 * channels)

def refold(columns, region_count, extent, channels):
    pieces = columns.reshape(region_count, extent, extent, 9, channels)
    padded = jnp.zeros((region_count, extent + 2, extent + 2, channels), columns.dtype)
    for row_off in range(3):
        for col_off in range(3):
            padded = padded.at[:, row_off:row_off + extent, col_off:col_off + extent, :].add(pieces[:, :, :, 3 * row_off + col_off, :])
    return padded[:, 1:-1, 1:-1, :]

def silu_slope(values):
    sigma = jax.nn.sigmoid(values)
    return sigma * (1.0 + values * (1.0 - sigma))

def region_pass(inputs, upstream, first_kernel, second_kernel):
    region_count = inputs.shape[0]
    extent = inputs.shape[1]
    channels = inputs.shape[3]
    first_flat = first_kernel.reshape(9 * channels, channels)
    second_flat = second_kernel.reshape(9 * channels, channels)
    input_cols = unfold(inputs)
    first_pre = jnp.dot(input_cols, first_flat, preferred_element_type=jnp.float32)
    hidden = jax.nn.silu(first_pre).astype(jnp.bfloat16)
    hidden_cols = unfold(hidden.reshape(region_count, extent, extent, channels))
    second_pre = jnp.dot(hidden_cols, second_flat, preferred_element_type=jnp.float32)
    second_delta = (upstream.reshape(-1, channels).astype(jnp.float32) * silu_slope(second_pre)).astype(jnp.bfloat16)
    second_raw = jnp.dot(hidden_cols.T, second_delta, preferred_element_type=jnp.float32)
    hidden_back = refold(jnp.dot(second_delta, second_flat.T, preferred_element_type=jnp.float32), region_count, extent, channels)
    first_delta = (hidden_back.reshape(-1, channels) * silu_slope(first_pre)).astype(jnp.bfloat16)
    first_raw = jnp.dot(input_cols.T, first_delta, preferred_element_type=jnp.float32)
    input_back = refold(jnp.dot(first_delta, first_flat.T, preferred_element_type=jnp.float32), region_count, extent, channels).astype(jnp.bfloat16)
    return (input_back, first_raw, second_raw)

def compact_plan(active, region_total):
    live_flags = active.reshape(-1)
    running = jnp.cumsum(live_flags.astype(jnp.int32), dtype=jnp.int32)
    region_ids = jnp.arange(region_total, dtype=jnp.int32)
    chosen = lax.optimization_barrier(jnp.sum((running[None, :] <= region_ids[:, None]).astype(jnp.int32), axis=1, dtype=jnp.int32))
    placed = jnp.maximum(running - 1, 0).astype(jnp.int32)
    return (chosen, placed, live_flags)

def scene_pass(scene_image, scene_upstream, counts, scene_grid, first_kernel, second_kernel):
    tile_images = scene_image.reshape(N_TILE, TH, TW, C)
    slot_ids = jnp.arange(CAP, dtype=jnp.int32)
    active = slot_ids[None, None, :] < counts[:, :, None]

    def owner_sample(members):
        owner_image, owner_grid, owner_active = members
        row_weights, col_weights = slot_weights(owner_grid, owner_active, TH, TW)
        return sample_blocks(owner_image, row_weights, col_weights)
    sent_blocks = lax.map(owner_sample, (tile_images, scene_grid, active))
    arrived = jnp.swapaxes(sent_blocks, 0, 1)
    reader_active = jnp.swapaxes(active, 0, 1)
    reader_upstream = scene_upstream.reshape(N_TILE, R_DEV, RES, RES, C)

    def reader_step(totals, members):
        reader_blocks, active_here, upstream_here = members
        chosen, placed, live_flags = compact_plan(active_here, R_DEV)
        inputs = jnp.take(reader_blocks.reshape(N_TILE * CAP, RES, RES, C), chosen, axis=0)
        input_back, first_raw, second_raw = region_pass(inputs, upstream_here, first_kernel, second_kernel)
        taken_back = jnp.take(input_back, placed, axis=0)
        slot_back = jnp.where(live_flags[:, None, None, None], taken_back, jnp.zeros_like(taken_back))
        return ((totals[0] + first_raw, totals[1] + second_raw), slot_back.reshape(N_TILE, CAP, RES, RES, C))
    zero_grad = jnp.zeros((9 * C, C), jnp.float32)
    sums, returned = lax.scan(reader_step, (zero_grad, zero_grad), (arrived, reader_active, reader_upstream))
    owner_back = jnp.swapaxes(returned, 0, 1)

    def owner_spread(members):
        owner_grads, owner_grid, owner_active = members
        row_weights, col_weights = slot_weights(owner_grid, owner_active, TH, TW)
        return spread_blocks(owner_grads, row_weights, col_weights)
    image_grads = lax.map(owner_spread, (owner_back, scene_grid, active))
    return (image_grads.reshape(N_TILE * TH, TW, C), sums[0], sums[1])

def reference(features, out_grad, pair_count, sample_grid, first_kernel, second_kernel):

    def one_scene(members):
        return scene_pass(members[0], members[1], members[2], members[3], first_kernel, second_kernel)
    image_grads, first_parts, second_parts = lax.map(one_scene, (features, out_grad, pair_count, sample_grid))
    grad_scale = 1.0 / math.sqrt(SCENES * N_TILE * R_DEV * RES * RES)
    first_grad = (lax.optimization_barrier(jnp.sum(first_parts, axis=0)) * grad_scale).reshape(3, 3, C, C)
    second_grad = (lax.optimization_barrier(jnp.sum(second_parts, axis=0)) * grad_scale).reshape(3, 3, C, C)
    return (image_grads, first_grad, second_grad)
```

```python
import functools
import math

import jax
import jax.numpy as jnp
from jax import lax
from jax.experimental import pallas as pl
from jax.experimental.pallas import tpu as pltpu
from jax.sharding import PartitionSpec as P

BF = jnp.bfloat16
F32 = jnp.float32
VMEM_BYTES = 60 * 1024 * 1024


def sigmoid(v):
    return jax.nn.sigmoid(v)


def keep_columns(shape, width, extent):
    rows = lax.broadcasted_iota(jnp.int32, shape, 0)
    return (rows % width) < extent


def store_shifted(ref, lead, width, values):
    rows, channels = values.shape
    shifted = (
        pltpu.roll(values, 1, 0),
        values,
        pltpu.roll(values, rows - 1, 0),
    )
    for part in range(3):
        block = shifted[part].astype(BF)
        ref[lead + (pl.ds(width, rows), pl.ds(part * channels, channels))] = block


def conv_taps(ref, lead, width, rows, weight_ref):
    total = None
    for tap in range(3):
        term = jnp.dot(
            ref[lead + (pl.ds(tap * width, rows), slice(None))],
            weight_ref[tap],
            preferred_element_type=F32,
        )
        total = term if total is None else total + term
    return total


def forward_kernel(
    extent, width, group,
    live_ref, low_ref, lw_ref, uw_ref,
    image_ref, mix_ref, w1_ref, w2_ref,
    x3_ref, h3_ref, s1_ref, s2_ref,
    stripe_ref,
):
    slot = pl.program_id(0)
    across = image_ref.shape[1]
    channels = image_ref.shape[2]
    rows = extent * width
    padded = x3_ref.shape[1]

    @pl.when(slot == 0)
    def _():
        stripe_ref[...] = jnp.zeros_like(stripe_ref)

    @pl.when(live_ref[slot] > 0)
    def _():
        for p in range(extent):
            low = low_ref[slot * extent + p]
            lower = image_ref[low].astype(F32) * lw_ref[slot * extent + p]
            upper = image_ref[low + 1].astype(F32) * uw_ref[slot * extent + p]
            stripe_ref[p * across : (p + 1) * across, :] = (lower + upper).astype(BF)
        x3_ref[0, 0:width, :] = jnp.zeros((width, 3 * channels), BF)
        start = width
        part_rows = group * width
        for half in range(stripe_ref.shape[0] // (group * across)):
            mixed = jnp.dot(
                mix_ref[0],
                stripe_ref[half * group * across : (half + 1) * group * across, :],
                preferred_element_type=F32,
            )
            count = min(part_rows, padded - start)
            for shift in range(3):
                x3_ref[0, start : start + count, shift * channels : (shift + 1) * channels] = mixed[
                    shift * part_rows : shift * part_rows + count
                ].astype(BF)
            start += count
        first_pre = conv_taps(x3_ref, (0,), width, rows, w1_ref)
        keep = keep_columns(first_pre.shape, width, extent)
        sigma = sigmoid(first_pre)
        hidden = jnp.where(keep, first_pre * sigma, 0.0)
        s1_ref[0] = jnp.where(keep, sigma * (1.0 + first_pre * (1.0 - sigma)), 0.0)
        h3_ref[0, 0:width, :] = jnp.zeros((width, 3 * channels), BF)
        h3_ref[0, width + rows : padded, :] = jnp.zeros((padded - width - rows, 3 * channels), BF)
        store_shifted(h3_ref, (0,), width, hidden)
        second_pre = conv_taps(h3_ref, (0,), width, rows, w2_ref)
        sigma = sigmoid(second_pre)
        s2_ref[0] = jnp.where(keep, sigma * (1.0 + second_pre * (1.0 - sigma)), 0.0)


def add_weight_grad(acc_ref, source, delta_ref, lead, width):
    rows, channels = source.shape
    flipped = source.T
    for row_off in range(3):
        part = jnp.dot(
            flipped,
            delta_ref[lead + (pl.ds((2 - row_off) * width, rows), slice(None))],
            preferred_element_type=F32,
        )
        for col_off in range(3):
            at = (2 - col_off) * channels
            acc_ref[3 * row_off + col_off] += part[:, at : at + channels]


def backward_kernel(
    extent, width,
    live_ref,
    up_ref, s2_ref, s1_ref, h_ref, x_ref, w2t_ref,
    d1_ref, g1_ref, g2_ref,
    d2_ref, acc1_ref, acc2_ref,
):
    slot = pl.program_id(0)
    rows = extent * width
    padded = d2_ref.shape[0]
    channels = up_ref.shape[2]

    @pl.when(slot == 0)
    def _():
        d2_ref[...] = jnp.zeros_like(d2_ref)
        acc1_ref[...] = jnp.zeros_like(acc1_ref)
        acc2_ref[...] = jnp.zeros_like(acc2_ref)

    @pl.when(live_ref[slot] > 0)
    def _():
        delta = up_ref[0].astype(F32) * s2_ref[0]
        store_shifted(d2_ref, (), width, delta)
        back = conv_taps(d2_ref, (), width, rows, w2t_ref)
        d1_ref[0, 0:width, :] = jnp.zeros((width, 3 * channels), BF)
        d1_ref[0, width + rows : padded, :] = jnp.zeros((padded - width - rows, 3 * channels), BF)
        store_shifted(d1_ref, (0,), width, back * s1_ref[0])
        add_weight_grad(acc2_ref, h_ref[0, width : width + rows, :], d2_ref, (), width)
        add_weight_grad(acc1_ref, x_ref[0, width : width + rows, :], d1_ref, (0,), width)

    @pl.when(slot == pl.num_programs(0) - 1)
    def _():
        g1_ref[...] = acc1_ref[...].astype(BF)
        g2_ref[...] = acc2_ref[...].astype(BF)


def spread_kernel(
    extent, width, group,
    live_ref, low_ref, lw_ref, uw_ref,
    d1_ref, mixt_ref, w1t_ref,
    grad_ref,
    sum_ref,
):
    slot = pl.program_id(0)
    rows = extent * width
    across = grad_ref.shape[1]

    @pl.when(slot == 0)
    def _():
        sum_ref[...] = jnp.zeros_like(sum_ref)

    @pl.when(live_ref[slot] > 0)
    def _():
        back = conv_taps(d1_ref, (0,), width, rows, w1t_ref).astype(BF)
        for first in range(0, extent, group):
            count = min(group, extent - first)
            stripes = jnp.dot(
                mixt_ref[0, 0 : count * across, 0 : count * width],
                back[first * width : (first + count) * width],
                preferred_element_type=F32,
            )
            stripes = stripes.astype(BF).astype(F32)
            for p in range(count):
                at = slot * extent + first + p
                low = low_ref[at]
                stripe = stripes[p * across : (p + 1) * across]
                sum_ref[low] += stripe * lw_ref[at]
                sum_ref[low + 1] += stripe * uw_ref[at]

    @pl.when(slot == pl.num_programs(0) - 1)
    def _():
        grad_ref[...] = sum_ref[...].astype(BF)


def compiler_params():
    return pltpu.CompilerParams(
        dimension_semantics=("arbitrary",), vmem_limit_bytes=VMEM_BYTES
    )


def whole(shape):
    return pl.BlockSpec(shape, lambda *_: (0,) * len(shape))


def by_slot(shape, column=0):
    return pl.BlockSpec((1,) + shape, lambda i, *_: (i, 0, column))


def exchange(value, axis, bit, size):
    return lax.ppermute(value, axis, [(i, i ^ bit) for i in range(size)])


def total_over(values, steps):
    acc = values.astype(F32)
    taken = []
    for axis, bit, size in steps:
        side = (lax.axis_index(axis) // bit) % 2
        half = acc.shape[0] // 2
        keep = lax.dynamic_slice_in_dim(acc, side * half, half, 0)
        send = lax.dynamic_slice_in_dim(acc, (1 - side) * half, half, 0).astype(BF)
        acc = keep + exchange(send, axis, bit, size).astype(F32)
        taken.append((axis, bit, size, side))
    out = acc.astype(BF)
    for axis, bit, size, side in reversed(taken):
        other = exchange(out, axis, bit, size)
        low = jnp.where(side == 0, out, other)
        high = jnp.where(side == 0, other, out)
        out = jnp.concatenate([low, high], axis=0)
    return out


def bits_of(axis, size):
    bit = 1
    while bit < size:
        yield (axis, bit, size)
        bit *= 2


def on_device(features, out_grad, pair_count, sample_grid, first_kernel, second_kernel):
    tiles = lax.axis_size("tile")
    groups = lax.axis_size("group")
    own = lax.axis_index("tile")
    image = features[0]
    height, across, channels = image.shape
    counts = pair_count[0]
    grid = sample_grid[0, 0]
    capacity = grid.shape[1]
    extent = grid.shape[3]
    upstream = out_grad[0]
    regions = upstream.shape[0]
    slots = tiles * capacity
    width = -(-(extent + 1) // 16) * 16
    padded = (extent + 2) * width
    rows = extent * width
    group = max(1, 256 // across)
    stripe_rows = -(-(extent + 1) // group) * group * across
    slot_ids = jnp.arange(capacity, dtype=jnp.int32)

    recv_counts = lax.dynamic_index_in_dim(counts, own, 1, keepdims=False)
    recv_live = (slot_ids[None, :] < recv_counts[:, None]).reshape(-1)
    placed = jnp.maximum(jnp.cumsum(recv_live.astype(jnp.int32), dtype=jnp.int32) - 1, 0)
    wide = jnp.pad(upstream, ((0, 0), (0, 0), (0, width - extent), (0, 0)))
    outgoing = jnp.take(wide.reshape(regions, rows, channels), placed, axis=0)
    outgoing = outgoing.reshape(tiles, capacity, rows, channels)
    up_slots = lax.all_to_all(outgoing, "tile", split_axis=0, concat_axis=0, tiled=True)
    up_slots = up_slots.reshape(slots, rows, channels)

    send_counts = lax.dynamic_index_in_dim(counts, own, 0, keepdims=False)
    live = (slot_ids[None, :] < send_counts[:, None]).astype(jnp.int32).reshape(-1)
    low = grid[..., 0, :].reshape(-1)
    upper = (grid[..., 1, :].astype(F32) / 16.0).reshape(-1)
    lower = 1.0 - upper

    col_low = grid[..., 2, :].reshape(slots, extent)
    col_up = grid[..., 3, :].reshape(slots, extent).astype(F32) / 16.0
    wide_low = jnp.pad(col_low, ((0, 0), (1, width - extent + 1)), constant_values=-8)
    wide_up = jnp.pad(col_up, ((0, 0), (1, width - extent + 1)))
    lows = jnp.stack([wide_low[:, b : b + width] for b in range(3)], axis=1)
    ups = jnp.stack([wide_up[:, b : b + width] for b in range(3)], axis=1)
    places = jnp.arange(across, dtype=jnp.int32)
    cols = jnp.where(places == lows[..., None], 1.0 - ups[..., None], 0.0)
    cols = cols + jnp.where(places == lows[..., None] + 1, ups[..., None], 0.0)
    same = jnp.eye(group, dtype=F32)
    mix = same[None, None, :, None, :, None] * cols[:, :, None, :, None, :]
    mix = mix.astype(BF).reshape(slots, 3 * group * width, group * across)
    centre = cols[:, 1]
    mix_t = same[None, :, None, :, None] * jnp.swapaxes(centre, 1, 2)[:, None, :, None, :]
    mix_t = mix_t.astype(BF).reshape(slots, group * across, group * width)

    w1 = first_kernel.reshape(3, 3 * channels, channels)
    w2 = second_kernel.reshape(3, 3 * channels, channels)

    def turned(kernel):
        return jnp.swapaxes(kernel[::-1, ::-1], 2, 3).reshape(3, 3 * channels, channels)

    wt_shape = (3, 3 * channels, channels)
    map3 = jax.ShapeDtypeStruct((slots, padded, 3 * channels), BF)
    slope = jax.ShapeDtypeStruct((slots, rows, channels), F32)
    x3, h3, s1, s2 = pl.pallas_call(
        functools.partial(forward_kernel, extent, width, group),
        out_shape=(map3, map3, slope, slope),
        grid_spec=pltpu.PrefetchScalarGridSpec(
            num_scalar_prefetch=4,
            grid=(slots,),
            in_specs=[
                whole(image.shape),
                by_slot(mix.shape[1:]),
                whole(wt_shape),
                whole(wt_shape),
            ],
            out_specs=[
                by_slot((padded, 3 * channels)),
                by_slot((padded, 3 * channels)),
                by_slot((rows, channels)),
                by_slot((rows, channels)),
            ],
            scratch_shapes=[pltpu.VMEM((stripe_rows, channels), BF)],
        ),
        compiler_params=compiler_params(),
        name="forward",
    )(live, low, lower, upper, image, mix, w1, w2)

    taps = jax.ShapeDtypeStruct((9, channels, channels), BF)
    d1, g1, g2 = pl.pallas_call(
        functools.partial(backward_kernel, extent, width),
        out_shape=(map3, taps, taps),
        grid_spec=pltpu.PrefetchScalarGridSpec(
            num_scalar_prefetch=1,
            grid=(slots,),
            in_specs=[
                by_slot((rows, channels)),
                by_slot((rows, channels)),
                by_slot((rows, channels)),
                by_slot((padded, channels), 1),
                by_slot((padded, channels), 1),
                whole(wt_shape),
            ],
            out_specs=[
                by_slot((padded, 3 * channels)),
                whole(taps.shape),
                whole(taps.shape),
            ],
            scratch_shapes=[
                pltpu.VMEM((padded, 3 * channels), BF),
                pltpu.VMEM((9, channels, channels), F32),
                pltpu.VMEM((9, channels, channels), F32),
            ],
        ),
        compiler_params=compiler_params(),
        name="backward",
    )(live, up_slots, s2, s1, h3, x3, turned(second_kernel))

    image_grad = pl.pallas_call(
        functools.partial(spread_kernel, extent, width, group),
        out_shape=jax.ShapeDtypeStruct(image.shape, BF),
        grid_spec=pltpu.PrefetchScalarGridSpec(
            num_scalar_prefetch=4,
            grid=(slots,),
            in_specs=[
                by_slot((padded, 3 * channels)),
                by_slot(mix_t.shape[1:]),
                whole(wt_shape),
            ],
            out_specs=whole(image.shape),
            scratch_shapes=[pltpu.VMEM(image.shape, F32)],
        ),
        compiler_params=compiler_params(),
        name="spread",
    )(live, low, lower, upper, d1, mix_t, turned(first_kernel))

    steps = list(bits_of("group", groups)) + list(bits_of("tile", tiles))
    scale = 1.0 / math.sqrt(groups * tiles * regions * extent * extent)
    both = jnp.concatenate([g1, g2], axis=0).reshape(2 * 9 * channels, channels)
    summed = total_over(both, steps).astype(F32) * scale
    summed = summed.reshape(2, 3, 3, channels, channels)
    return (image_grad[None], summed[0], summed[1])


def solution(mesh):
    return jax.shard_map(
        on_device,
        mesh=mesh,
        in_specs=(
            P("group", "tile", None, None),
            P("group", "tile", None, None, None),
            P("group", None, None),
            P("group", "tile", None, None, None, None),
            P(),
            P(),
        ),
        out_specs=(P("group", "tile", None, None), P(), P()),
        check_vma=False,
    )
```

```python
import functools
import math

import jax
import jax.numpy as jnp
from jax import lax
from jax.experimental import pallas as pl
from jax.experimental.pallas import tpu as pltpu
from jax.sharding import PartitionSpec as P

BF = jnp.bfloat16
F32 = jnp.float32
VMEM_BYTES = 60 * 1024 * 1024
FAR = 1.0e6
AXES = ("tile", "group")


def iota(shape, dim):
    return lax.broadcasted_iota(jnp.int32, shape, dim)


def shifted_copies(values):
    rows = values.shape[0]
    return (pltpu.roll(values, 1, 0), values, pltpu.roll(values, rows - 1, 0))


def store_shifted(ref, slot, start, values):
    rows, channels = values.shape
    for part, block in enumerate(shifted_copies(values)):
        ref[slot, start : start + rows, part * channels : (part + 1) * channels] = block.astype(BF)


def conv_taps(ref, start, width, rows, weight_ref):
    count = ref.shape[0]
    total = None
    for tap in range(3):
        at = start + tap * width
        left = ref[:, at : at + rows, :].reshape(count * rows, ref.shape[2])
        term = jnp.dot(left, weight_ref[tap], preferred_element_type=F32)
        total = term if total is None else total + term
    return total


def hat(base_ref, index_ref, start, step):
    place = start + step * index_ref[...]
    return jnp.maximum(1.0 - jnp.abs(base_ref[...] - place) * 0.0625, 0.0).astype(BF)


def row_place(meta_ref, slot, p):
    at = meta_ref[4 * slot] + meta_ref[4 * slot + 1] * p
    return at // 16, (at % 16).astype(F32) * 0.0625


def forward_kernel(
    extent, width, group, capacity,
    live_ref, meta_ref,
    image_ref, w1_ref, w2_ref,
    xt_ref, ht_ref, s1_ref, s2_ref, w1t_ref, w2t_ref,
    stripe_ref, x3_ref, h3_ref, base_ref, index_ref,
):
    step = pl.program_id(0)
    across = image_ref.shape[1]
    channels = image_ref.shape[2]
    rows = extent * width
    padded = x3_ref.shape[1]
    part_rows = group * width

    @pl.when(step == 0)
    def _():
        stripe_ref[...] = jnp.zeros_like(stripe_ref)
        x3_ref[...] = jnp.zeros_like(x3_ref)
        h3_ref[...] = jnp.zeros_like(h3_ref)
        shape = base_ref.shape
        row, lane = iota(shape, 0), iota(shape, 1)
        index = row % width + row // part_rows - 1
        fits = (lane // across == (row % part_rows) // width) & (index >= 0) & (index < extent)
        fits = fits & (row % width < extent)
        base_ref[...] = jnp.where(fits, (16 * (lane % across)).astype(F32), FAR)
        index_ref[...] = index.astype(F32)
        for source, target in ((w1_ref, w1t_ref), (w2_ref, w2t_ref)):
            for a in range(3):
                for b in range(3):
                    tap = source[2 - a, (2 - b) * channels : (3 - b) * channels, :]
                    target[a, b * channels : (b + 1) * channels, :] = tap.T

    busy = live_ref[step * capacity]
    for g in range(1, capacity):
        busy = busy + live_ref[step * capacity + g]

    @pl.when(busy > 0)
    def _():
        for g in range(capacity):
            slot = step * capacity + g
            alive = live_ref[slot].astype(F32)
            for p in range(extent):
                low, share = row_place(meta_ref, slot, p)
                lower = image_ref[low].astype(F32) * ((1.0 - share) * alive)
                upper = image_ref[low + 1].astype(F32) * (share * alive)
                stripe_ref[g, p * across : (p + 1) * across, :] = (lower + upper).astype(BF)
            mix = hat(
                base_ref, index_ref,
                meta_ref[4 * slot + 2].astype(F32), meta_ref[4 * slot + 3].astype(F32),
            )
            start = width
            for half in range(stripe_ref.shape[1] // (group * across)):
                mixed = jnp.dot(
                    mix,
                    stripe_ref[g, half * group * across : (half + 1) * group * across, :],
                    preferred_element_type=F32,
                )
                count = min(part_rows, padded - start)
                for b in range(3):
                    block = mixed[b * part_rows : b * part_rows + count]
                    x3_ref[g, start : start + count, b * channels : (b + 1) * channels] = (
                        block.astype(BF)
                    )
                start += count
        pre = conv_taps(x3_ref, 0, width, rows, w1_ref)
        keep = (iota((rows, channels), 0) % width) < extent
        for g in range(capacity):
            value = pre[g * rows : (g + 1) * rows]
            sigma = jax.nn.sigmoid(value)
            s1_ref[g] = jnp.where(keep, sigma * (1.0 + value * (1.0 - sigma)), 0.0)
            store_shifted(h3_ref, g, width, jnp.where(keep, value * sigma, 0.0))
            xt_ref[g] = x3_ref[g].T
        pre = conv_taps(h3_ref, 0, width, rows, w2_ref)
        for g in range(capacity):
            value = pre[g * rows : (g + 1) * rows]
            sigma = jax.nn.sigmoid(value)
            s2_ref[g] = jnp.where(keep, sigma * (1.0 + value * (1.0 - sigma)), 0.0)
            ht_ref[g] = h3_ref[g].T


def add_weight_grad(acc_ref, source_ref, delta_ref, width):
    count, deep, padded = source_ref.shape
    channels = deep // 3
    left = jnp.concatenate([source_ref[g] for g in range(count)], axis=1)
    for a in range(3):
        at = (2 - a) * width
        right = delta_ref[:, at : at + padded, channels : 2 * channels]
        part = jnp.dot(left, right.reshape(count * padded, channels), preferred_element_type=F32)
        acc_ref[a * deep : (a + 1) * deep, :] += part


def backward_kernel(
    extent, width, first_step, parts, carried, last, blocks,
    live_ref, order_ref, *refs,
):
    up_refs, refs = refs[:parts], refs[parts:]
    s2_ref, s1_ref, ht_ref, xt_ref, w2t_ref, *refs = refs
    if carried:
        in1_ref, in2_ref, *refs = refs
    d1_ref, *refs = refs
    if last:
        sums_ref, *refs = refs
    else:
        out1_ref, out2_ref, *refs = refs
    up_ref, d2_ref, d1s_ref, acc1_ref, acc2_ref = refs
    step = pl.program_id(0)
    rows = extent * width
    capacity = up_ref.shape[0]
    channels = up_ref.shape[2]

    @pl.when(step == 0)
    def _():
        up_ref[...] = jnp.zeros_like(up_ref)
        d2_ref[...] = jnp.zeros_like(d2_ref)
        d1s_ref[...] = jnp.zeros_like(d1s_ref)
        if carried:
            acc1_ref[...] = in1_ref[...]
            acc2_ref[...] = in2_ref[...]
        else:
            acc1_ref[...] = jnp.zeros_like(acc1_ref)
            acc2_ref[...] = jnp.zeros_like(acc2_ref)

    busy = live_ref[(first_step + step) * capacity]
    for g in range(1, capacity):
        busy = busy + live_ref[(first_step + step) * capacity + g]

    for part in range(parts):
        @pl.when((busy > 0) & (step == part))
        def _():
            for g in range(capacity):
                for i in range(extent):
                    up_ref[g, i * width : i * width + extent, :] = up_refs[part][g, i]

    @pl.when(busy > 0)
    def _():
        for g in range(capacity):
            store_shifted(d2_ref, g, 2 * width, up_ref[g].astype(F32) * s2_ref[g])
        back = conv_taps(d2_ref, width, width, rows, w2t_ref)
        for g in range(capacity):
            store_shifted(d1s_ref, g, 2 * width, back[g * rows : (g + 1) * rows] * s1_ref[g])
        add_weight_grad(acc2_ref, ht_ref, d2_ref, width)
        add_weight_grad(acc1_ref, xt_ref, d1s_ref, width)
        d1_ref[...] = d1s_ref[:, width : width + d1_ref.shape[1], :]

    @pl.when(step == pl.num_programs(0) - 1)
    def _():
        if last:
            size = acc1_ref.shape[0] // blocks
            for k in range(blocks):
                at = pl.multiple_of((order_ref[0] ^ k) * size, size)
                for j, (zero, one) in enumerate(
                    ((acc1_ref, acc2_ref), (acc2_ref, acc1_ref))
                ):
                    @pl.when(order_ref[1] == 0)
                    def _():
                        sums_ref[j, k * size : (k + 1) * size, :] = zero[pl.ds(at, size)].astype(BF)

                    @pl.when(order_ref[1] != 0)
                    def _():
                        sums_ref[j, k * size : (k + 1) * size, :] = one[pl.ds(at, size)].astype(BF)
        else:
            out1_ref[...] = acc1_ref[...]
            out2_ref[...] = acc2_ref[...]


def spread_kernel(
    extent, width, group, capacity,
    live_ref, meta_ref,
    d1_ref, w1t_ref,
    grad_ref,
    sum_ref, base_ref, index_ref,
):
    step = pl.program_id(0)
    rows = extent * width
    across = grad_ref.shape[1]

    @pl.when(step == 0)
    def _():
        sum_ref[...] = jnp.zeros_like(sum_ref)
        shape = base_ref.shape
        row, lane = iota(shape, 0), iota(shape, 1)
        index = lane % width
        fits = (row // across == lane // width) & (index < extent)
        base_ref[...] = jnp.where(fits, (16 * (row % across)).astype(F32), FAR)
        index_ref[...] = index.astype(F32)

    busy = live_ref[step * capacity]
    for g in range(1, capacity):
        busy = busy + live_ref[step * capacity + g]

    @pl.when(busy > 0)
    def _():
        back = conv_taps(d1_ref, 0, width, rows, w1t_ref).astype(BF)
        for g in range(capacity):
            slot = step * capacity + g
            alive = live_ref[slot].astype(F32)
            mix = hat(
                base_ref, index_ref,
                meta_ref[4 * slot + 2].astype(F32), meta_ref[4 * slot + 3].astype(F32),
            )
            for first in range(0, extent, group):
                count = min(group, extent - first)
                at = g * rows + first * width
                stripes = jnp.dot(
                    mix[0 : count * across, 0 : count * width],
                    back[at : at + count * width],
                    preferred_element_type=F32,
                ).astype(BF).astype(F32)
                for p in range(count):
                    low, share = row_place(meta_ref, slot, first + p)
                    stripe = stripes[p * across : (p + 1) * across]
                    sum_ref[low] += stripe * ((1.0 - share) * alive)
                    sum_ref[low + 1] += stripe * (share * alive)

    @pl.when(step == pl.num_programs(0) - 1)
    def _():
        grad_ref[...] = sum_ref[...].astype(BF)


def finish_kernel(scale, inner, order_ref, own_ref, other_ref, first_ref, second_ref):
    size = own_ref.shape[0] // inner
    low = order_ref[0] % inner

    def place(source, target):
        for k in range(inner):
            at = pl.multiple_of((low ^ k) * size, size)
            target[k * size : (k + 1) * size, :] = source[pl.ds(at, size)].astype(F32) * scale

    @pl.when(order_ref[1] == 0)
    def _():
        place(own_ref, first_ref)
        place(other_ref, second_ref)

    @pl.when(order_ref[1] != 0)
    def _():
        place(other_ref, first_ref)
        place(own_ref, second_ref)


def compiler_params():
    return pltpu.CompilerParams(
        dimension_semantics=("arbitrary",), vmem_limit_bytes=VMEM_BYTES
    )


def whole(shape):
    return pl.BlockSpec(shape, lambda *_: (0,) * len(shape))


def stepped(shape, base=0):
    return pl.BlockSpec(shape, lambda i, *_: (i + base,) + (0,) * (len(shape) - 1))


def partner(value, mask, total):
    return lax.ppermute(value, AXES, [(i, i ^ mask) for i in range(total)])


def masks_of(bits):
    found = [0]
    for bit in bits:
        found = found + [m | bit for m in found]
    return found


def bits_below(size):
    return [1 << n for n in range(size.bit_length() - 1)]


def plan_stages(tiles, groups):
    group_bits = bits_below(groups)
    tile_bits = [bit * groups for bit in bits_below(tiles)]
    bits = group_bits + tile_bits
    head, rest = bits[:1], bits[1:]
    stages = []
    if len(group_bits) > 1 and tile_bits:
        joined = [tile_bits[0], group_bits[-1]]
        stages.append(joined)
        rest = [bit for bit in rest if bit not in joined]
    stages.extend([bit] for bit in rest)
    return head, stages


def reduce_stage(value, bits, total):
    masks = masks_of(bits)
    size = value.shape[0] // len(masks)
    got = [
        partner(value[k * size : (k + 1) * size], masks[k], total) for k in range(1, len(masks))
    ]
    acc = value[:size].astype(F32)
    for piece in got:
        acc = acc + piece.astype(F32)
    return acc.astype(BF)


def gather_stage(value, bits, total):
    masks = masks_of(bits)
    return jnp.concatenate([value] + [partner(value, m, total) for m in masks[1:]], axis=0)


def on_device(features, out_grad, pair_count, sample_grid, first_kernel, second_kernel):
    tiles = lax.axis_size("tile")
    groups = lax.axis_size("group")
    total = tiles * groups
    own = lax.axis_index("tile")
    image = features[0]
    height, across, channels = image.shape
    counts = pair_count[0]
    grid = sample_grid[0, 0]
    capacity = grid.shape[1]
    extent = grid.shape[3]
    upstream = out_grad[0]
    regions = upstream.shape[0]
    slots = tiles * capacity
    width = -(-(extent + 1) // 16) * 16
    padded = (extent + 2) * width
    rows = extent * width
    deep = 3 * channels
    group = max(1, 256 // across)
    stripe_rows = -(-(extent + 1) // group) * group * across
    slot_ids = jnp.arange(capacity, dtype=jnp.int32)
    peers = jnp.arange(tiles, dtype=jnp.int32) ^ own

    recv_counts = lax.dynamic_index_in_dim(counts, own, 1, keepdims=False)
    before = jnp.sum(
        jnp.where(jnp.arange(tiles)[None, :] < peers[:, None], recv_counts[None, :], 0),
        axis=1, dtype=jnp.int32,
    )
    source = jnp.minimum(before[:, None] + slot_ids[None, :], regions - 1).reshape(-1)
    outgoing = upstream.at[source].get(mode="promise_in_bounds")
    outgoing = outgoing.reshape((tiles, capacity) + upstream.shape[1:])
    arrived = [outgoing[0]]
    for k in range(1, tiles):
        arrived.append(
            lax.ppermute(outgoing[k], "tile", [(i, i ^ k) for i in range(tiles)])
        )

    send_counts = lax.dynamic_index_in_dim(counts, own, 0, keepdims=False)
    live = (slot_ids[None, :] < send_counts[peers][:, None]).astype(jnp.int32).reshape(-1)
    mine = grid[peers]
    starts = 16 * mine[:, :, 0::2, 0] + mine[:, :, 1::2, 0]
    nexts = 16 * mine[:, :, 0::2, 1] + mine[:, :, 1::2, 1]
    meta = jnp.stack([starts, nexts - starts], axis=-1).reshape(-1).astype(jnp.int32)

    w1 = first_kernel.reshape(3, deep, channels)
    w2 = second_kernel.reshape(3, deep, channels)
    turned = jax.ShapeDtypeStruct(w1.shape, BF)
    flipped = jax.ShapeDtypeStruct((slots, deep, padded), BF)
    slope = jax.ShapeDtypeStruct((slots, rows, channels), F32)
    map_spec = (capacity, padded, deep)
    flip_spec = (capacity, deep, padded)
    slope_spec = (capacity, rows, channels)
    mix_rows = 3 * group * width
    xt, ht, s1, s2, w1t, w2t = pl.pallas_call(
        functools.partial(forward_kernel, extent, width, group, capacity),
        out_shape=(flipped, flipped, slope, slope, turned, turned),
        grid_spec=pltpu.PrefetchScalarGridSpec(
            num_scalar_prefetch=2,
            grid=(tiles,),
            in_specs=[whole(image.shape), whole(w1.shape), whole(w2.shape)],
            out_specs=[
                stepped(flip_spec), stepped(flip_spec), stepped(slope_spec), stepped(slope_spec),
                whole(w1.shape), whole(w2.shape),
            ],
            scratch_shapes=[
                pltpu.VMEM((capacity, stripe_rows, channels), BF),
                pltpu.VMEM(map_spec, BF),
                pltpu.VMEM(map_spec, BF),
                pltpu.VMEM((mix_rows, group * across), F32),
                pltpu.VMEM((mix_rows, group * across), F32),
            ],
        ),
        compiler_params=compiler_params(),
        name="forward",
    )(live, meta, image, w1, w2)

    head, stages = plan_stages(tiles, groups)
    blocks = 1
    for bits in stages:
        blocks *= 2 ** len(bits)
    relative = (9 * channels) % (16 * blocks) == 0 and blocks >= 4
    flat = lax.axis_index("tile") * groups + lax.axis_index("group")
    if relative:
        order = jnp.int32(0)
        for bits in stages:
            for bit in reversed(bits):
                order = 2 * order + (flat // bit) % 2
        order = jnp.stack([order, (flat // head[0]) % 2]).astype(jnp.int32)
    else:
        blocks = 1
        order = jnp.zeros((2,), jnp.int32)

    def backward(first, parts, carried, last):
        acc = jax.ShapeDtypeStruct((9 * channels, channels), F32)
        d1_shape = jax.ShapeDtypeStruct((parts * capacity, padded, deep), BF)
        if last:
            sums = jax.ShapeDtypeStruct((2, 9 * channels, channels), BF)
            outs, out_specs = (sums,), [whole(sums.shape)]
        else:
            outs, out_specs = (acc, acc), [whole(acc.shape)] * 2
        ups = arrived[first : first + parts]
        return pl.pallas_call(
            functools.partial(
                backward_kernel, extent, width, first, parts, bool(carried), last, blocks
            ),
            out_shape=(d1_shape,) + outs,
            grid_spec=pltpu.PrefetchScalarGridSpec(
                num_scalar_prefetch=2,
                grid=(parts,),
                in_specs=[whole(up.shape) for up in ups]
                + [
                    stepped(slope_spec, first), stepped(slope_spec, first),
                    stepped(flip_spec, first), stepped(flip_spec, first),
                    whole(w2t.shape),
                ]
                + [whole(acc.shape) for _ in carried],
                out_specs=[stepped(map_spec)] + out_specs,
                scratch_shapes=[
                    pltpu.VMEM(slope_spec, BF),
                    pltpu.VMEM((capacity, padded + 2 * width, deep), BF),
                    pltpu.VMEM((capacity, padded + 2 * width, deep), BF),
                    pltpu.VMEM(acc.shape, F32),
                    pltpu.VMEM(acc.shape, F32),
                ],
            ),
            compiler_params=compiler_params(),
            name="backward",
        )(live, order, *ups, s2, s1, ht, xt, w2t, *carried)

    late = max(1, tiles // 4)
    early_d1, acc1, acc2 = backward(0, tiles - late, (), False)
    late_d1, sums = backward(tiles - late, late, (acc1, acc2), True)

    d1 = jnp.concatenate([early_d1, late_d1], axis=0)

    def spread(d1):
        return pl.pallas_call(
            functools.partial(spread_kernel, extent, width, group, capacity),
            out_shape=jax.ShapeDtypeStruct(image.shape, BF),
            grid_spec=pltpu.PrefetchScalarGridSpec(
                num_scalar_prefetch=2,
                grid=(tiles,),
                in_specs=[stepped(map_spec), whole(w1t.shape)],
                out_specs=whole(image.shape),
                scratch_shapes=[
                    pltpu.VMEM(image.shape, F32),
                    pltpu.VMEM((group * across, group * width), F32),
                    pltpu.VMEM((group * across, group * width), F32),
                ],
            ),
            compiler_params=compiler_params(),
            name="spread",
        )(live, meta, d1, w1t)

    scale = 1.0 / math.sqrt(total * regions * extent * extent)
    if not relative:
        image_grad = spread(d1)
        summed = lax.psum(sums, AXES).astype(F32) * scale
        first_grad, second_grad = summed[0], summed[1]
    else:
        got = partner(sums[1], head[0], total)
        value = (sums[0].astype(F32) + got.astype(F32)).astype(BF)
        value, d1 = lax.optimization_barrier((value, d1))
        image_grad = spread(d1)
        value = reduce_stage(value, stages[0], total)
        value, image_grad = lax.optimization_barrier((value, image_grad))
        for bits in stages[1:]:
            value = reduce_stage(value, bits, total)
        for bits in reversed(stages):
            value = gather_stage(value, bits, total)
        other = partner(value, head[0], total)
        inner = 4
        outer = blocks // inner
        piece = (9 * channels // outer, channels)
        full = jax.ShapeDtypeStruct((9 * channels, channels), F32)
        first_grad, second_grad = pl.pallas_call(
            functools.partial(finish_kernel, scale, inner),
            out_shape=(full, full),
            grid_spec=pltpu.PrefetchScalarGridSpec(
                num_scalar_prefetch=1,
                grid=(outer,),
                in_specs=[
                    pl.BlockSpec(piece, lambda i, order: (i ^ (order[0] // inner), 0))
                ] * 2,
                out_specs=[pl.BlockSpec(piece, lambda i, order: (i, 0))] * 2,
            ),
            compiler_params=compiler_params(),
            name="finish",
        )(order, value, other)
    shape = (3, 3, channels, channels)
    return (image_grad[None], first_grad.reshape(shape), second_grad.reshape(shape))


def solution(mesh):
    return jax.shard_map(
        on_device,
        mesh=mesh,
        in_specs=(
            P("group", "tile", None, None),
            P("group", "tile", None, None, None),
            P("group", None, None),
            P("group", "tile", None, None, None, None),
            P(),
            P(),
        ),
        out_specs=(P("group", "tile", None, None), P(), P()),
        check_vma=False,
    )
```

```python
import functools
import math

import jax
import jax.numpy as jnp
from jax import lax
from jax.experimental import pallas as pl
from jax.experimental.pallas import tpu as pltpu
from jax.sharding import PartitionSpec as P

BF = jnp.bfloat16
F32 = jnp.float32
MIB = 1024 * 1024
AXES = ("tile", "group")


def iota(shape, dim):
    return lax.broadcasted_iota(jnp.int32, shape, dim)


def shifted_copies(values):
    rows = values.shape[0]
    return (pltpu.roll(values, 1, 0), values, pltpu.roll(values, rows - 1, 0))


def store_shifted(ref, slot, start, values):
    rows, channels = values.shape
    for part, block in enumerate(shifted_copies(values)):
        ref[slot, start : start + rows, part * channels : (part + 1) * channels] = block.astype(BF)


def conv_taps(ref, slot, count, start, width, rows, weight_ref):
    total = None
    for tap in range(3):
        at = start + tap * width
        left = ref[slot : slot + count, at : at + rows, :].reshape(count * rows, ref.shape[2])
        term = jnp.dot(left, weight_ref[tap], preferred_element_type=F32)
        total = term if total is None else total + term
    return total


def hat(row_index, lane_place, start, step, fits):
    place = (start + step * row_index).astype(F32)
    weight = jnp.maximum(1.0 - jnp.abs(lane_place.astype(F32) * 16.0 - place) * 0.0625, 0.0)
    return jnp.where(fits, weight, 0.0)


def slot_scalars(counts_ref, grid_ref, own, slot, capacity):
    peer = own ^ (slot // capacity)
    member = slot % capacity
    alive = (member < counts_ref[own, peer]).astype(jnp.int32)

    def track(which):
        first = 16 * grid_ref[peer, member, which, 0] + grid_ref[peer, member, which + 1, 0]
        second = 16 * grid_ref[peer, member, which, 1] + grid_ref[peer, member, which + 1, 1]
        return first, second - first

    return alive, track(0), track(2)


def group_busy(counts_ref, own, first, count, capacity):
    busy = jnp.int32(0)
    for slot in range(count):
        peer = own ^ ((first + slot) // capacity)
        busy = busy + ((first + slot) % capacity < counts_ref[own, peer]).astype(jnp.int32)
    return busy > 0


def dispatch_kernel(capacity, counts_ref, up_ref, *refs):
    outs, sems = refs[:-1], refs[-1]
    own = lax.axis_index("tile")
    tiles = counts_ref.shape[0]
    regions = up_ref.shape[0]
    copies = []
    for k in range(tiles):
        peer = own ^ k
        before = jnp.int32(0)
        for o in range(tiles):
            before = before + jnp.where(o < peer, counts_ref[o, own], 0)
        for s in range(capacity):
            copy = pltpu.make_async_copy(
                up_ref.at[jnp.minimum(before + s, regions - 1)],
                outs[k].at[s],
                sems.at[k * capacity + s],
            )
            copy.start()
            copies.append(copy)
    for copy in copies:
        copy.wait()


def forward_kernel(
    extent, width, capacity,
    counts_ref, grid_ref,
    image_ref, w1_ref, w2_ref,
    x_ref, h_ref, s1_ref, s2_ref, w1t_ref, w2t_ref,
    x3_ref, h3_ref,
):
    step = pl.program_id(0)
    own = lax.axis_index("tile")
    across = image_ref.shape[1]
    channels = image_ref.shape[2]
    rows = extent * width
    count, padded = x3_ref.shape[:2]

    @pl.when(step == 0)
    def _():
        x3_ref[...] = jnp.zeros_like(x3_ref)
        h3_ref[...] = jnp.zeros_like(h3_ref)
        for source, target in ((w1_ref, w1t_ref), (w2_ref, w2t_ref)):
            for a in range(3):
                for b in range(3):
                    tap = source[2 - a, (2 - b) * channels : (3 - b) * channels, :]
                    target[a, b * channels : (b + 1) * channels, :] = tap.T

    @pl.when(group_busy(counts_ref, own, step * count, count, capacity))
    def _():
        shape = (3 * width, 2 * across)
        row, lane = iota(shape, 0), iota(shape, 1)
        index = row % width + row // width - 1
        fits = (index >= 0) & (index < extent) & (row % width < extent)
        upper = lane >= across
        keep = (iota((rows, channels), 0) % width) < extent
        half = 2 if count % 2 == 0 else 1

        def sample(g):
            alive, across_rows, across_cols = slot_scalars(
                counts_ref, grid_ref, own, step * count + g, capacity
            )
            mix = hat(
                index, lane % across, across_cols[0], across_cols[1], fits
            ) * alive.astype(F32)
            for p in range(extent):
                at = across_rows[0] + across_rows[1] * p
                low = at >> 4
                share = (at & 15).astype(F32) * 0.0625
                weight = (mix * jnp.where(upper, share, 1.0 - share)).astype(BF)
                pair = image_ref[pl.ds(low, 2)].reshape(2 * across, channels)
                mixed = jnp.dot(weight, pair, preferred_element_type=F32).astype(BF)
                for b in range(3):
                    x3_ref[
                        g,
                        (p + 1) * width : (p + 2) * width,
                        b * channels : (b + 1) * channels,
                    ] = mixed[b * width : (b + 1) * width]

        def sloped(value):
            sigma = jax.nn.sigmoid(value)
            return sigma, jnp.where(keep, sigma * (1.0 + value * (1.0 - sigma)), 0.0)

        firsts = range(0, count, half)
        pres = []
        for first in firsts:
            for g in range(first, first + half):
                sample(g)
            pres.append(conv_taps(x3_ref, first, half, 0, width, rows, w1_ref))
        nexts = []
        for first, pre in zip(firsts, pres):
            for g in range(first, first + half):
                value = pre[(g - first) * rows : (g - first + 1) * rows]
                sigma, s1_ref[g] = sloped(value)
                store_shifted(h3_ref, g, width, jnp.where(keep, value * sigma, 0.0))
            nexts.append(conv_taps(h3_ref, first, half, 0, width, rows, w2_ref))
        for first, pre in zip(firsts, nexts):
            for g in range(first, first + half):
                _, s2_ref[g] = sloped(pre[(g - first) * rows : (g - first + 1) * rows])
        x_ref[...] = x3_ref[:, :, channels : 2 * channels]
        h_ref[...] = h3_ref[:, :, channels : 2 * channels]


def add_weight_grad(acc_ref, source_ref, delta_ref, width):
    count, padded, channels = source_ref.shape
    for a in range(3):
        at = (2 - a) * width
        part = None
        for g in range(count):
            term = lax.dot_general(
                source_ref[g],
                delta_ref[g, at : at + padded, :],
                (((0,), (0,)), ((), ())),
                preferred_element_type=F32,
            )
            part = term if part is None else part + term
        for b in range(3):
            tap = 3 * a + b
            at_b = (2 - b) * channels
            acc_ref[tap * channels : (tap + 1) * channels, :] += part[:, at_b : at_b + channels]


def backward_kernel(
    extent, width, first_step, parts, capacity, carried, last, ordering,
    counts_ref, *refs,
):
    up_refs, refs = refs[:parts], refs[parts:]
    s2_ref, s1_ref, h_ref, x_ref, w2t_ref, *refs = refs
    if carried:
        in1_ref, in2_ref, _, *refs = refs
    d1_ref, *refs = refs
    if last:
        near_ref, away_ref, *refs = refs
    else:
        out1_ref, out2_ref, *refs = refs
    up_ref, d2_ref, d1s_ref, acc1_ref, acc2_ref, sems = refs
    step = pl.program_id(0)
    own = lax.axis_index("tile")
    rows = extent * width
    count = up_ref.shape[0]
    members = count // capacity

    loads = []
    if carried:
        loads = [
            pltpu.make_async_copy(in1_ref, acc1_ref, sems.at[0]),
            pltpu.make_async_copy(in2_ref, acc2_ref, sems.at[1]),
        ]

    @pl.when(step == 0)
    def _():
        for load in loads:
            load.start()
        up_ref[...] = jnp.zeros_like(up_ref)
        d2_ref[...] = jnp.zeros_like(d2_ref)
        d1s_ref[...] = jnp.zeros_like(d1s_ref)
        if not carried:
            acc1_ref[...] = jnp.zeros_like(acc1_ref)
            acc2_ref[...] = jnp.zeros_like(acc2_ref)

    busy = group_busy(counts_ref, own, (first_step + step) * count, count, capacity)

    for part in range(parts):
        @pl.when(busy & (step == part // members))
        def _():
            for g in range(capacity):
                for i in range(extent):
                    up_ref[
                        part % members * capacity + g, i * width : i * width + extent, :
                    ] = up_refs[part][g, i]

    @pl.when(busy)
    def _():
        for g in range(count):
            store_shifted(d2_ref, g, 2 * width, up_ref[g].astype(F32) * s2_ref[g])
        back = conv_taps(d2_ref, 0, count, width, width, rows, w2t_ref)
        for g in range(count):
            store_shifted(d1s_ref, g, 2 * width, back[g * rows : (g + 1) * rows] * s1_ref[g])

    @pl.when(step == 0)
    def _():
        for load in loads:
            load.wait()

    @pl.when(busy)
    def _():
        add_weight_grad(acc2_ref, h_ref, d2_ref, width)
        add_weight_grad(acc1_ref, x_ref, d1s_ref, width)
        d1_ref[...] = d1s_ref[:, width : width + d1_ref.shape[1], :]

    @pl.when(step == pl.num_programs(0) - 1)
    def _():
        if last:
            order, side, blocks = ordering()
            size = acc1_ref.shape[0] // blocks

            def place(source_ref, target_ref):
                for k in range(blocks):
                    at = pl.multiple_of((order ^ k) * size, size)
                    target_ref[k * size : (k + 1) * size, :] = source_ref[pl.ds(at, size)].astype(BF)

            @pl.when(side == 0)
            def _():
                place(acc1_ref, near_ref)
                place(acc2_ref, away_ref)

            @pl.when(side != 0)
            def _():
                place(acc2_ref, near_ref)
                place(acc1_ref, away_ref)
        else:
            out1_ref[...] = acc1_ref[...]
            out2_ref[...] = acc2_ref[...]


def spread_kernel(
    extent, width, capacity,
    counts_ref, grid_ref,
    d1_ref, w1t_ref,
    grad_ref,
    sum_ref,
):
    step = pl.program_id(0)
    own = lax.axis_index("tile")
    rows = extent * width
    across, channels = grad_ref.shape[1:]
    count = d1_ref.shape[0]

    @pl.when(step == 0)
    def _():
        sum_ref[...] = jnp.zeros_like(sum_ref)

    @pl.when(group_busy(counts_ref, own, step * count, count, capacity))
    def _():
        shape = (2 * across, width)
        row, lane = iota(shape, 0), iota(shape, 1)
        upper = row >= across
        back = conv_taps(d1_ref, 0, count, 0, width, rows, w1t_ref).astype(BF)
        for g in range(count):
            alive, across_rows, across_cols = slot_scalars(
                counts_ref, grid_ref, own, step * count + g, capacity
            )
            mix = hat(
                lane, row % across, across_cols[0], across_cols[1], lane < extent
            ) * alive.astype(F32)
            for p in range(extent):
                at = across_rows[0] + across_rows[1] * p
                low = at >> 4
                share = (at & 15).astype(F32) * 0.0625
                weight = (mix * jnp.where(upper, share, 1.0 - share)).astype(BF)
                spread = jnp.dot(
                    weight,
                    back[g * rows + p * width : g * rows + (p + 1) * width],
                    preferred_element_type=F32,
                )
                sum_ref[pl.ds(low, 2)] += spread.reshape(2, across, channels)

    @pl.when(step == pl.num_programs(0) - 1)
    def _():
        grad_ref[...] = sum_ref[...].astype(BF)


def finish_kernel(scale, inner, order_ref, own_ref, other_ref, first_ref, second_ref):
    size = own_ref.shape[0] // inner
    low = order_ref[0] % inner

    def place(source, target):
        for k in range(inner):
            at = pl.multiple_of((low ^ k) * size, size)
            target[k * size : (k + 1) * size, :] = source[pl.ds(at, size)].astype(F32) * scale

    @pl.when(order_ref[1] == 0)
    def _():
        place(own_ref, first_ref)
        place(other_ref, second_ref)

    @pl.when(order_ref[1] != 0)
    def _():
        place(other_ref, first_ref)
        place(own_ref, second_ref)


def compiler_params(mib):
    return pltpu.CompilerParams(
        dimension_semantics=("arbitrary",), vmem_limit_bytes=mib * MIB
    )


def whole(shape):
    return pl.BlockSpec(shape, lambda *_: (0,) * len(shape))


def stepped(shape, base=0):
    return pl.BlockSpec(shape, lambda i, *_: (i + base,) + (0,) * (len(shape) - 1))


def partner(value, mask, total):
    return lax.ppermute(value, AXES, [(i, i ^ mask) for i in range(total)])


def masks_of(bits):
    found = [0]
    for bit in bits:
        found = found + [m | bit for m in found]
    return found


def bits_below(size):
    return [1 << n for n in range(size.bit_length() - 1)]


def plan_stages(tiles, groups):
    group_bits = bits_below(groups)
    tile_bits = [bit * groups for bit in bits_below(tiles)]
    bits = group_bits + tile_bits
    head, rest = bits[:1], bits[1:]
    stages = []
    if len(group_bits) > 1 and tile_bits:
        joined = [tile_bits[0], group_bits[-1]]
        stages.append(joined)
        rest = [bit for bit in rest if bit not in joined]
    stages.extend([bit] for bit in rest)
    return head, stages


def reduce_stage(value, bits, total):
    masks = masks_of(bits)
    size = value.shape[0] // len(masks)
    got = [
        partner(value[k * size : (k + 1) * size], masks[k], total) for k in range(1, len(masks))
    ]
    acc = value[:size].astype(F32)
    for piece in got:
        acc = acc + piece.astype(F32)
    return acc.astype(BF)


def gather_stage(value, bits, total):
    masks = masks_of(bits)
    return jnp.concatenate([value] + [partner(value, m, total) for m in masks[1:]], axis=0)


def on_device(features, out_grad, pair_count, sample_grid, first_kernel, second_kernel):
    tiles = lax.axis_size("tile")
    groups = lax.axis_size("group")
    total = tiles * groups
    image = features[0]
    height, across, channels = image.shape
    counts = pair_count[0]
    grid = sample_grid[0, 0]
    capacity = grid.shape[1]
    extent = grid.shape[3]
    upstream = out_grad[0]
    regions = upstream.shape[0]
    slots = tiles * capacity
    width = -(-(extent + 1) // 16) * 16
    padded = (extent + 2) * width
    rows = extent * width
    deep = 3 * channels
    count = capacity * (2 if tiles % 2 == 0 else 1)
    members = count // capacity
    anywhere = pl.BlockSpec(memory_space=pl.ANY)

    share = jax.ShapeDtypeStruct((capacity,) + upstream.shape[1:], BF)
    outgoing = pl.pallas_call(
        functools.partial(dispatch_kernel, capacity),
        out_shape=(share,) * tiles,
        grid_spec=pltpu.PrefetchScalarGridSpec(
            num_scalar_prefetch=1,
            grid=(1,),
            in_specs=[anywhere],
            out_specs=[anywhere] * tiles,
            scratch_shapes=[pltpu.SemaphoreType.DMA((slots,))],
        ),
        compiler_params=compiler_params(2),
        name="dispatch",
    )(counts, upstream)
    arrived = [outgoing[0]]
    for k in range(1, tiles):
        arrived.append(
            lax.ppermute(outgoing[k], "tile", [(i, i ^ k) for i in range(tiles)])
        )

    w1 = first_kernel.reshape(3, deep, channels)
    w2 = second_kernel.reshape(3, deep, channels)
    turned = jax.ShapeDtypeStruct(w1.shape, BF)
    plain = jax.ShapeDtypeStruct((slots, padded, channels), BF)
    slope = jax.ShapeDtypeStruct((slots, rows, channels), F32)
    map_spec = (count, padded, deep)
    plain_spec = (count, padded, channels)
    slope_spec = (count, rows, channels)
    x, h, s1, s2, w1t, w2t = pl.pallas_call(
        functools.partial(forward_kernel, extent, width, capacity),
        out_shape=(plain, plain, slope, slope, turned, turned),
        grid_spec=pltpu.PrefetchScalarGridSpec(
            num_scalar_prefetch=2,
            grid=(slots // count,),
            in_specs=[whole(image.shape), whole(w1.shape), whole(w2.shape)],
            out_specs=[
                stepped(plain_spec), stepped(plain_spec), stepped(slope_spec), stepped(slope_spec),
                whole(w1.shape), whole(w2.shape),
            ],
            scratch_shapes=[pltpu.VMEM(map_spec, BF), pltpu.VMEM(map_spec, BF)],
        ),
        compiler_params=compiler_params(34),
        name="forward",
    )(counts, grid, image, w1, w2)

    head, stages = plan_stages(tiles, groups)
    blocks = 1
    for bits in stages:
        blocks *= 2 ** len(bits)
    relative = (9 * channels) % (16 * blocks) == 0 and blocks >= 4

    def ordering():
        if not relative:
            return jnp.int32(0), jnp.int32(0), 1
        flat = lax.axis_index("tile") * groups + lax.axis_index("group")
        order = jnp.int32(0)
        for bits in stages:
            for bit in reversed(bits):
                order = 2 * order + (flat // bit) % 2
        return order, (flat // head[0]) % 2, blocks

    acc = jax.ShapeDtypeStruct((9 * channels, channels), F32)
    half_sum = jax.ShapeDtypeStruct((9 * channels, channels), BF)
    d1_shape = jax.ShapeDtypeStruct((slots, padded, deep), BF)

    def backward(first, parts, carried, last):
        base = first // members
        outs = (half_sum, half_sum) if last else (acc, acc)
        ups = arrived[first : first + parts]
        operands = (counts, *ups, s2, s1, h, x, w2t, *carried)
        return pl.pallas_call(
            functools.partial(
                backward_kernel, extent, width, base, parts, capacity,
                bool(carried), last, ordering,
            ),
            out_shape=(d1_shape,) + outs,
            grid_spec=pltpu.PrefetchScalarGridSpec(
                num_scalar_prefetch=1,
                grid=(parts // members,),
                in_specs=[whole(up.shape) for up in ups]
                + [
                    stepped(slope_spec, base), stepped(slope_spec, base),
                    stepped(plain_spec, base), stepped(plain_spec, base),
                    whole(w2t.shape),
                ]
                + [anywhere for _ in carried],
                out_specs=[stepped(map_spec, base)] + [whole(acc.shape)] * 2,
                scratch_shapes=[
                    pltpu.VMEM(slope_spec, BF),
                    pltpu.VMEM((count, padded + 2 * width, deep), BF),
                    pltpu.VMEM((count, padded + 2 * width, deep), BF),
                    pltpu.VMEM(acc.shape, F32),
                    pltpu.VMEM(acc.shape, F32),
                    pltpu.SemaphoreType.DMA((2,)),
                ],
            ),
            input_output_aliases={len(operands) - 1: 0} if carried else {},
            compiler_params=compiler_params(44),
            name="backward",
        )(*operands)

    late = max(members, tiles // 4)
    d1, acc1, acc2 = backward(0, tiles - late, (), False)
    d1, near, away = backward(tiles - late, late, (acc1, acc2, d1), True)

    def spread(d1):
        return pl.pallas_call(
            functools.partial(spread_kernel, extent, width, capacity),
            out_shape=jax.ShapeDtypeStruct(image.shape, BF),
            grid_spec=pltpu.PrefetchScalarGridSpec(
                num_scalar_prefetch=2,
                grid=(slots // count,),
                in_specs=[stepped(map_spec), whole(w1t.shape)],
                out_specs=whole(image.shape),
                scratch_shapes=[pltpu.VMEM(image.shape, F32)],
            ),
            compiler_params=compiler_params(24),
            name="spread",
        )(counts, grid, d1, w1t)

    scale = 1.0 / math.sqrt(total * regions * extent * extent)
    if not relative:
        image_grad = spread(d1)
        first_grad = lax.psum(near, AXES).astype(F32) * scale
        second_grad = lax.psum(away, AXES).astype(F32) * scale
    else:
        got = partner(away, head[0], total)
        value = (near.astype(F32) + got.astype(F32)).astype(BF)
        value, d1 = lax.optimization_barrier((value, d1))
        image_grad = spread(d1)
        value = reduce_stage(value, stages[0], total)
        value, image_grad = lax.optimization_barrier((value, image_grad))
        for bits in stages[1:]:
            value = reduce_stage(value, bits, total)
        for bits in reversed(stages):
            value = gather_stage(value, bits, total)
        other = partner(value, head[0], total)
        order, side, _ = ordering()
        order = jnp.stack([order, side]).astype(jnp.int32)
        inner = 2
        outer = blocks // inner
        piece = (9 * channels // outer, channels)
        full = jax.ShapeDtypeStruct((9 * channels, channels), F32)
        first_grad, second_grad = pl.pallas_call(
            functools.partial(finish_kernel, scale, inner),
            out_shape=(full, full),
            grid_spec=pltpu.PrefetchScalarGridSpec(
                num_scalar_prefetch=1,
                grid=(outer,),
                in_specs=[
                    pl.BlockSpec(piece, lambda i, order: (i ^ (order[0] // inner), 0))
                ] * 2,
                out_specs=[pl.BlockSpec(piece, lambda i, order: (i, 0))] * 2,
            ),
            compiler_params=compiler_params(16),
            name="finish",
        )(order, value, other)
    shape = (3, 3, channels, channels)
    return (image_grad[None], first_grad.reshape(shape), second_grad.reshape(shape))


def solution(mesh):
    return jax.shard_map(
        on_device,
        mesh=mesh,
        in_specs=(
            P("group", "tile", None, None),
            P("group", "tile", None, None, None),
            P("group", None, None),
            P("group", "tile", None, None, None, None),
            P(),
            P(),
        ),
        out_specs=(P("group", "tile", None, None), P(), P()),
        check_vma=False,
    )
```
